256 devices in a mesh: user: 8 (over y, x_lo), item: 32 (over z, x_hi, core).
Axes of the slice: x: 4 (x_hi: 2, x_lo: 2; x = x_hi * 2 + x_lo), y: 4, z: 8, core: 2. Of those that a mesh axis runs over, the one named last changes fastest.
Arguments:
- user_panel: bfloat16 [2048, 1024], P(('user', 'item')), may hold values from -6 to 6
- attr_panel: bfloat16 [2048, 1024], P(('user', 'item')), may hold values from -6 to 6
- user_blocks: bfloat16 [128, 4096, 128], P('user', 'item'), may hold values from -6 to 6
- user_rows: int32 [128, 32], P('user', 'item'), may hold values from 0 to 1
- user_cols: int32 [128, 32], P('user', 'item'), may hold values from 0 to 24
- attr_blocks: bfloat16 [128, 4096, 128], P('user', 'item'), may hold values from -6 to 6
- attr_rows: int32 [128, 32], P('user', 'item'), may hold values from 0 to 1
- attr_cols: int32 [128, 32], P('user', 'item'), may hold values from 0 to 24
Outputs:
- band_tail: float32 [1024, 102400], P('user', 'item')
- band_self: float32 [1024, 1024], P('user', 'item')
The draws below stay inside these ranges and needn't reach their ends.
All inputs are finite; a program needn't handle non-finite values.
Results may differ from the reference program's by a relative error of at most 0.012.
Values may be sent and summed in bfloat16 or wider, within the bound.
A program may use at most 64 MiB of HBM per device.

```python
import math
import jax
import jax.numpy as jnp
import numpy as np
from jax import lax

BLOCK = 128
BAND = 1024
ITEM_DEV = 3200
UB = 2
AB = 2
NB = 16
NA = 16
USERS = 2048
ATTRS = 2048
N_USER = 8
N_ITEM = 32


def place_ends(result, key, least, top_value):
    place = [jax.random.randint(jax.random.fold_in(key, axis), (), 0, length) for axis, length in enumerate(result.shape)]
    longest = result.shape.index(max(result.shape))
    neighbour = place[:longest] + [(place[longest] + 1) % result.shape[longest]] + place[longest + 1:]
    return result.at[tuple(place)].set(least).at[tuple(neighbour)].set(top_value)


def levels(key, dims, cuts, smallest, high):
    def one(position, blocks):
        steps = jax.random.uniform(jax.random.fold_in(jax.random.fold_in(key, 6), position), (blocks,), jnp.float32, smallest / len(cuts), high / len(cuts))
        return jnp.repeat(jnp.exp(steps), dims[position] // blocks).reshape((-1,) + (1,) * (len(dims) - position - 1))

    factor_of = one(*cuts[0])
    for cut in cuts[1:]:
        factor_of = factor_of * one(*cut)
    return factor_of


def rank_table(number_of, skew):
    weights = [(1 << 20) // math.isqrt(grade ** skew) + 1 for grade in range(1, number_of + 1)]
    width = 1 + sum(weights) // (1 << 30)
    return np.cumsum(np.array([max(1, weight // width) for weight in weights]))


def ranked(own_key, dims, amount, skew):
    listing = rank_table(amount, skew)
    pick = jax.random.randint(jax.random.fold_in(own_key, 1), dims, 0, int(listing[amount - 1]))
    standing = jnp.searchsorted(jnp.asarray(listing, jnp.int32), pick, side="right")
    return jax.random.permutation(jax.random.fold_in(own_key, 2), amount)[standing].astype(jnp.int32)


def normal_values(own_key, extent, scale, reach, cuts=(), held_as=jnp.bfloat16):
    array = jax.random.normal(own_key, extent, jnp.float32) * scale
    if len(cuts) > 0:
        array = levels(own_key, extent, cuts, -0.22, 0.18) * array
    return jnp.clip(array, min=-reach, max=reach).astype(held_as)


def setup_inputs(seed: int = 0) -> dict:
    arg_keys = jax.random.split(jax.random.key(seed), 9)
    user_panel = normal_values(arg_keys[0], (USERS, BAND), 1.0, 6.0, ((0, 256),))
    attr_panel = normal_values(arg_keys[1], (ATTRS, BAND), 1.0, 6.0, ((0, 256),))
    user_blocks = normal_values(arg_keys[2], (NB * N_USER, N_ITEM * BLOCK, BLOCK), 1.0, 6.0, ((0, 8), (1, 32)))
    user_rows = place_ends(ranked(arg_keys[3], (NB * N_USER, N_ITEM), UB, 2), jax.random.fold_in(arg_keys[3], 3), 0, UB - 1).astype(jnp.int32)
    user_cols = place_ends(jax.random.randint(arg_keys[4], (NB * N_USER, N_ITEM), 0, ITEM_DEV // BLOCK), jax.random.fold_in(arg_keys[4], 1), 0, (ITEM_DEV // BLOCK) - 1).astype(jnp.int32)
    attr_blocks = normal_values(arg_keys[5], (NA * N_USER, N_ITEM * BLOCK, BLOCK), 1.0, 6.0, ((0, 8), (1, 32)))
    attr_rows = place_ends(ranked(arg_keys[6], (NA * N_USER, N_ITEM), AB, 2), jax.random.fold_in(arg_keys[6], 3), 0, AB - 1).astype(jnp.int32)
    attr_cols = place_ends(jax.random.randint(arg_keys[7], (NA * N_USER, N_ITEM), 0, ITEM_DEV // BLOCK), jax.random.fold_in(arg_keys[7], 1), 0, (ITEM_DEV // BLOCK) - 1).astype(jnp.int32)
    return dict(user_panel=user_panel, attr_panel=attr_panel, user_blocks=user_blocks, user_rows=user_rows, user_cols=user_cols, attr_blocks=attr_blocks, attr_rows=attr_rows, attr_cols=attr_cols)


alpha_weight = 0.5
ridge = 1.0

def dense_shard(blocks, rows, cols, row_blocks):
    item_blocks = ITEM_DEV // BLOCK
    count = blocks.shape[0]
    pieces = blocks.astype(jnp.float32).reshape(count, N_ITEM, BLOCK, BLOCK)
    item_ids = lax.broadcasted_iota(jnp.int32, (count, N_ITEM), 1)
    start = jnp.zeros((row_blocks, BLOCK, N_ITEM, item_blocks, BLOCK), jnp.float32)
    dense = start.at[rows.astype(jnp.int32), :, item_ids, cols.astype(jnp.int32), :].add(pieces)
    return dense.reshape(row_blocks * BLOCK, N_ITEM * ITEM_DEV).astype(jnp.bfloat16)

def rounded(value):
    low = lax.optimization_barrier(value.astype(jnp.bfloat16))
    return low.astype(jnp.float32)

def reference(user_panel, attr_panel, user_blocks, user_rows, user_cols, attr_blocks, attr_rows, attr_cols):
    users_dev = UB * BLOCK
    attrs_dev = AB * BLOCK
    blocks_dev = UB * 8
    attr_dev_blocks = AB * 8
    gram_tail = jnp.zeros((BAND, N_ITEM * ITEM_DEV), jnp.float32)
    gram_self = jnp.zeros((BAND, BAND), jnp.float32)
    for shard in range(N_USER):
        upan = user_panel[shard * users_dev:(shard + 1) * users_dev]
        apan = attr_panel[shard * attrs_dev:(shard + 1) * attrs_dev]
        ublk = user_blocks[shard * blocks_dev:(shard + 1) * blocks_dev]
        urow = user_rows[shard * blocks_dev:(shard + 1) * blocks_dev]
        ucol = user_cols[shard * blocks_dev:(shard + 1) * blocks_dev]
        ablk = attr_blocks[shard * attr_dev_blocks:(shard + 1) * attr_dev_blocks]
        arow = attr_rows[shard * attr_dev_blocks:(shard + 1) * attr_dev_blocks]
        acol = attr_cols[shard * attr_dev_blocks:(shard + 1) * attr_dev_blocks]
        user_dense = dense_shard(ublk, urow, ucol, UB)
        attr_dense = dense_shard(ablk, arow, acol, AB)
        tail = jnp.dot(upan.T, user_dense, preferred_element_type=jnp.float32) + alpha_weight * jnp.dot(apan.T, attr_dense, preferred_element_type=jnp.float32)
        selfpart = jnp.dot(upan.T, upan, preferred_element_type=jnp.float32) + alpha_weight * jnp.dot(apan.T, apan, preferred_element_type=jnp.float32)
        gram_tail = gram_tail + rounded(tail)
        gram_self = gram_self + rounded(selfpart)
    upf = user_panel.astype(jnp.float32)
    apf = attr_panel.astype(jnp.float32)
    weight = lax.optimization_barrier(jnp.sum(upf * upf, axis=0)) + alpha_weight * lax.optimization_barrier(jnp.sum(apf * apf, axis=0))
    scale = lax.rsqrt(weight + ridge)
    band_tail = gram_tail * scale[:, None]
    diag = jnp.eye(BAND, dtype=jnp.bool_)
    band_self = jnp.where(diag, jnp.float32(0.0), gram_self * scale[:, None])
    return (band_tail, band_self)
```

```python
import jax
import jax.numpy as jnp
from jax import lax
from jax.experimental import pallas as pl
from jax.experimental.pallas import tpu as pltpu
from jax.sharding import PartitionSpec as P

SIDE = 128
BLOCKS = 16
COLS = 25
ZERO = 64
NA, NB = 7, 6
NK = NA + NB
MESH = pl.DeviceIdType.MESH
F32, BF16 = jnp.float32, jnp.bfloat16


def merge_kernel(up, ap, ub, ab, ur, uc, ar, ac, u_out, blk_out, map_out, acc):
    for t, pan in enumerate((up, ap)):
        for m in range(8):
            u_out[m % 2, t, :, (m // 2) * 128:(m // 2 + 1) * 128] = pan[:, m * 128:(m + 1) * 128]
    for row in range(4):
        for c in range(COLS + 1):
            map_out[row, c] = ZERO
    for t, (blk, rows, cols) in enumerate(((ub, ur, uc), (ab, ar, ac))):
        twin = [jnp.int32(0)] * BLOCKS
        for q in range(BLOCKS - 1, -1, -1):
            row, c = t * 2 + rows[q, 0], cols[q, 0]
            twin[q] = map_out[row, c]
            map_out[row, c] = t * BLOCKS + q
        for q in range(BLOCKS):
            blk_out[t * BLOCKS + q] = blk[q]
        for q in range(BLOCKS - 1):
            row, c = t * 2 + rows[q, 0], cols[q, 0]
            first = jnp.logical_and(map_out[row, c] == t * BLOCKS + q, twin[q] != ZERO)

            @pl.when(first)
            def _(q=q, t=t, blk=blk, rows=rows, cols=cols):
                acc[...] = blk[q].astype(F32)

                def add(o, carry):
                    same = jnp.logical_and(rows[o, 0] == rows[q, 0], cols[o, 0] == cols[q, 0])

                    @pl.when(same)
                    def _():
                        acc[...] += blk[o].astype(F32)

                    return carry

                lax.fori_loop(q + 1, BLOCKS, add, 0)
                blk_out[t * BLOCKS + q] = acc[...].astype(BF16)


def gram_kernel(u_ref, blk_ref, map_ref, tail_ref, self_ref, w_ref,
                g, xb, smap, vmap, xrel, tall, pt, srhs, rhs,
                far, near_p, near_m, keep_p, keep_m, own, rfar_p, rfar_m, rp, rm,
                wrow, wsend, wrelay, wp, wm,
                loc, xs, xr, zs, zr, ss, sr, bs, br, es, er, fs, fr, ns, nr, vs, vr):
    user, item = lax.axis_index("user"), lax.axis_index("item")
    y, a = user // 2, user % 2
    z, h, c = item // 4, (item // 2) % 2, item % 2
    x = h * 2 + a

    def dev(dy=0, dx=0, dz=0, flip=False):
        yy, xx, zz = (y + dy + 4) % 4, (x + dx + 4) % 4, (z + dz + 8) % 8
        cc = 1 - c if flip else c
        return (yy * 2 + xx % 2, zz * 4 + (xx // 2) * 2 + cc)

    partner = (y * 2 + (1 - a), item)

    def send(src, dst, ssem, rsem, to):
        return pltpu.make_async_remote_copy(
            src_ref=src, dst_ref=dst, send_sem=ssem, recv_sem=rsem,
            device_id=to, device_id_type=MESH)

    barrier = pltpu.get_barrier_semaphore()
    for peer in (dev(dy=1), dev(dy=-1), dev(dx=1), dev(dx=-1), dev(dz=1), dev(dz=-1), dev(flip=True)):
        pl.semaphore_signal(barrier, inc=1, device_id=peer, device_id_type=MESH)
    pl.semaphore_wait(barrier, 7)

    h_left, h_right = ((x + 3) % 4) // 2, ((x + 1) % 4) // 2
    x_copies = [
        send(u_ref.at[1 - a], g.at[z, c, 1, h], xs.at[0], xr.at[0], dev(dx=1)),
        send(u_ref.at[1 - a], g.at[z, c, 1, h], xs.at[1], xr.at[1], dev(dx=-1)),
        send(u_ref.at[a, 0], xrel.at[0], xs.at[2], xr.at[2], dev(dx=1)),
        send(u_ref.at[a, 1], xrel.at[1], xs.at[3], xr.at[3], dev(dx=-1)),
    ]
    for cp in (x_copies[2], x_copies[3], x_copies[0], x_copies[1]):
        cp.start()
    map_copy = send(map_ref, vmap, bs.at[4], br.at[4], partner)
    map_copy.start()
    b_copies = [send(blk_ref.at[pl.ds(8 * i, 8)], xb.at[pl.ds(32 + 8 * i, 8)], bs.at[i], br.at[i], partner)
                for i in range(4)]
    for cp in b_copies:
        cp.start()
    own_u = pltpu.make_async_copy(u_ref.at[a], g.at[z, c, 0, h], loc.at[0])
    own_b = pltpu.make_async_copy(blk_ref, xb.at[pl.ds(0, 32)], loc.at[1])
    own_m = pltpu.make_async_copy(map_ref, smap.at[0], loc.at[2])
    for cp in (own_u, own_b, own_m):
        cp.start()
    xb[ZERO] = jnp.zeros((SIDE, SIDE), BF16)
    x_copies[2].wait_recv()
    fwd0 = send(xrel.at[0], g.at[z, c, 0, h_left, 0], xs.at[4], xr.at[4], dev(dx=1))
    fwd0.start()
    x_copies[3].wait_recv()
    fwd1 = send(xrel.at[1], g.at[z, c, 0, h_right, 1], xs.at[5], xr.at[5], dev(dx=-1))
    fwd1.start()
    x_copies[0].wait_recv()
    x_copies[1].wait_recv()

    def ring(step, sub, up):
        zz = (z + 8 - step) % 8 if up else (z + step) % 8
        i = (step if up else 4 + step) * 2 + sub
        return send(g.at[zz, c, sub], g.at[zz, c, sub], zs.at[i], zr.at[i], dev(dz=1 if up else -1))

    def share(zz, i):
        return send(g.at[zz, c], g.at[zz, c], ss.at[i], sr.at[i], dev(flip=True))

    ups = [[ring(k, s, True) for s in range(2)] for k in range(4)]
    downs = [[ring(k, s, False) for s in range(2)] for k in range(3)]
    ups[0][1].start()
    downs[0][1].start()
    own_u.wait()
    fwd0.wait_recv()
    fwd1.wait_recv()
    ups[0][0].start()
    downs[0][0].start()
    shares = [share(z, 0)]
    shares[0].start()
    for k in range(4):
        for s in (1, 0):
            ups[k][s].wait_recv()
            if k < 3:
                ups[k + 1][s].start()
                downs[k][s].wait_recv()
                if k < 2:
                    downs[k + 1][s].start()
        shares.append(share((z + 7 - k) % 8, 1 + k))
        shares[-1].start()
        if k < 3:
            shares.append(share((z + 1 + k) % 8, 5 + k))
            shares[-1].start()
    for cp in shares:
        cp.wait_recv()

    for rel in range(4):
        wrow[rel] = jnp.zeros((8, SIDE), F32)
    for side in range(2):
        for t in range(2):
            for i in range(32):
                tall[i * 8:(i + 1) * 8, :] = g[i // 4, i % 2, side, (i // 2) % 2, t].astype(F32)
            first = side * 512 + t * 256
            for rel in range(4):
                yb = (y + rel) % 4
                v = tall[:, pl.ds(pl.multiple_of(yb * SIDE, SIDE), SIDE)]
                squares = jnp.sum(v * v, axis=0, keepdims=True)
                vt = v.T
                if t == 1:
                    squares, vt = squares * 0.5, vt * 0.5
                wrow[rel] += jnp.broadcast_to(squares, (8, SIDE))
                pt[rel * SIDE:(rel + 1) * SIDE, first:first + 256] = vt.astype(BF16)

            @pl.when(z % 2 == a)
            def _():
                srhs[first:first + 256, :] = tall[:, pl.ds(pl.multiple_of((z // 2) * SIDE, SIDE), SIDE)].astype(BF16)

    wsend[0] = wrow[2]
    wsend[1] = wrow[3]
    w_far = send(wsend.at[0], wrelay, vs.at[0], vr.at[0], dev(dy=1))
    w_near_m = send(wsend.at[1], wm, vs.at[1], vr.at[1], dev(dy=-1))
    w_far.start()
    w_near_m.start()

    map_copy.wait_recv()
    got_map = pltpu.make_async_copy(vmap, smap.at[1], loc.at[3])
    got_map.start()
    own_b.wait()
    own_m.wait()
    got_map.wait()
    for cp in b_copies:
        cp.wait_recv()

    e_copies = [send(srhs.at[pl.ds(s * 512, 512)], srhs.at[pl.ds((1 - s) * 512, 512)], es.at[s], er.at[s], partner)
                for s in range(2)]

    @pl.when(z % 2 == a)
    def _():
        for cp in e_copies:
            cp.start()

    def far_copy(k, up):
        if up:
            return send(far.at[k], rfar_p.at[k], fs.at[k], fr.at[k], dev(dy=1))
        return send(far.at[k], rfar_m.at[k - NA], fs.at[k], fr.at[k], dev(dy=-1))

    def near_copy(k, up):
        if up:
            return send(near_p.at[k], rp.at[k], ns.at[k], nr.at[k], dev(dy=1))
        return send(near_m.at[k], rm.at[k], ns.at[NK + k], nr.at[NK + k], dev(dy=-1))

    def compute(k, up, last=False):
        for j in range(1 if last else 2):
            for p in range(8):
                at = smap[p // 4, p % 4, 2 * k + j]
                if p >= 4:
                    at = jnp.where(at == ZERO, ZERO, at + 32)
                rhs[p * SIDE:(p + 1) * SIDE, j * SIDE:(j + 1) * SIDE] = xb[at]
        if last:
            rhs[:, SIDE:2 * SIDE] = srhs[...]
        terms = jnp.dot(pt[...], rhs[...], preferred_element_type=F32)
        far[k] = terms[256:384].astype(BF16)
        far_copy(k, up).start()
        own[k] = terms[0:128]
        if up:
            near_m[k] = terms[384:512].astype(BF16)
            near_copy(k, False).start()
            keep_p[k] = terms[128:256]
        else:
            near_p[k] = terms[128:256].astype(BF16)
            near_copy(k, True).start()
            keep_m[k - NA] = terms[384:512]

    def both(i, carry):
        compute(i, True)
        compute(NA + i, False)
        return carry

    lax.fori_loop(0, NB - 1, both, 0)
    compute(NB - 1, True)
    compute(NA - 1, True)

    @pl.when(z % 2 != a)
    def _():
        for cp in e_copies:
            cp.wait_recv()

    compute(NK - 1, False, last=True)

    w_far.wait_recv()
    wsend[2] = wrow[1] + wrelay[...]
    w_near_p = send(wsend.at[2], wp, vs.at[2], vr.at[2], dev(dy=1))
    w_near_p.start()

    def relay_up(k):
        far_copy(k, True).wait_recv()
        near_p[k] = (keep_p[k] + rfar_p[k].astype(F32)).astype(BF16)
        near_copy(k, True).start()

    def relay_down(k):
        far_copy(k, False).wait_recv()
        near_m[k] = (keep_m[k - NA] + rfar_m[k - NA].astype(F32)).astype(BF16)
        near_copy(k, False).start()

    def relay(i, carry):
        relay_up(i)
        relay_down(NA + i)
        return carry

    lax.fori_loop(0, NB, relay, 0)
    relay_up(NA - 1)

    def total(k):
        near_copy(k, True).wait_recv()
        near_copy(k, False).wait_recv()
        return own[k] + (rp[k].astype(F32) + rm[k].astype(F32))

    def finish(k, carry):
        tail_ref[:, pl.ds(pl.multiple_of(k * 256, 256), 256)] = total(k)
        return carry

    lax.fori_loop(0, NK - 1, finish, 0)
    end = total(NK - 1)
    tail_ref[:, (NK - 1) * 256:] = end[:, :SIDE]
    self_ref[...] = end[:, SIDE:]
    w_near_m.wait_recv()
    w_near_p.wait_recv()
    w_ref[...] = wrow[0] + (wp[...] + wm[...])

    for cp in x_copies + [fwd0, fwd1] + shares + b_copies + [map_copy, w_far, w_near_m, w_near_p]:
        cp.wait_send()
    for cp in ups + downs:
        for part in cp:
            part.wait_send()

    @pl.when(z % 2 == a)
    def _():
        for cp in e_copies:
            cp.wait_send()

    def drain_a(k, carry):
        far_copy(k, True).wait_send()
        near_copy(k, True).wait_send()
        near_copy(k, False).wait_send()
        return carry

    def drain_b(k, carry):
        far_copy(k, False).wait_send()
        near_copy(k, True).wait_send()
        near_copy(k, False).wait_send()
        return carry

    lax.fori_loop(0, NA, drain_a, 0)
    lax.fori_loop(NA, NK, drain_b, 0)


def local(up, ap, ub, ur, uc, ab, ar, ac):
    vmem, smem = pl.BlockSpec(memory_space=pltpu.VMEM), pl.BlockSpec(memory_space=pltpu.SMEM)
    hbm = pl.BlockSpec(memory_space=pl.ANY)
    shape = jax.ShapeDtypeStruct
    u, blk, cells = pl.pallas_call(
        merge_kernel,
        out_shape=(shape((2, 2, 8, 512), BF16), shape((32, SIDE, SIDE), BF16), shape((8, 128), jnp.int32)),
        in_specs=[vmem] * 4 + [smem] * 4,
        out_specs=(vmem, vmem, smem),
        scratch_shapes=[pltpu.VMEM((SIDE, SIDE), F32)],
        name="merge",
    )(up, ap, ub, ab, ur, uc, ar, ac)
    vm, dma = pltpu.VMEM, pltpu.SemaphoreType.DMA
    width = (NK * 2 - 1) * SIDE
    tail, own_self, weight = pl.pallas_call(
        gram_kernel,
        out_shape=(shape((SIDE, width), F32), shape((SIDE, SIDE), F32), shape((8, SIDE), F32)),
        in_specs=[hbm, hbm, hbm],
        out_specs=(vmem, vmem, vmem),
        scratch_shapes=[
            vm((8, 2, 2, 2, 2, 8, 512), BF16),
            vm((ZERO + 1, SIDE, SIDE), BF16),
            pltpu.SMEM((2, 8, 128), jnp.int32),
            vm((8, 128), jnp.int32),
            vm((2, 8, 512), BF16),
            vm((256, 512), F32),
            vm((512, 1024), BF16),
            vm((1024, SIDE), BF16),
            vm((1024, 256), BF16),
            vm((NK, SIDE, 256), BF16),
            vm((NK, SIDE, 256), BF16),
            vm((NK, SIDE, 256), BF16),
            vm((NA, SIDE, 256), F32),
            vm((NB, SIDE, 256), F32),
            vm((NK, SIDE, 256), F32),
            vm((NA, SIDE, 256), BF16),
            vm((NB, SIDE, 256), BF16),
            vm((NK, SIDE, 256), BF16),
            vm((NK, SIDE, 256), BF16),
            vm((4, 8, SIDE), F32),
            vm((3, 8, SIDE), F32),
            vm((8, SIDE), F32),
            vm((8, SIDE), F32),
            vm((8, SIDE), F32),
            dma((4,)), dma((6,)), dma((6,)), dma((14,)), dma((14,)), dma((8,)), dma((8,)),
            dma((5,)), dma((5,)), dma((2,)), dma((2,)), dma((NK,)), dma((NK,)),
            dma((2 * NK,)), dma((2 * NK,)), dma((3,)), dma((3,)),
        ],
        compiler_params=pltpu.CompilerParams(
            collective_id=0, has_side_effects=True, vmem_limit_bytes=48 * 1024 * 1024),
        name="gram",
    )(u, blk, cells)
    user, item = lax.axis_index("user"), lax.axis_index("item")
    scale = lax.rsqrt(weight[0] + 1.0)[:, None]
    part = lax.dynamic_slice_in_dim(own_self, (item % 4) * 32, 32, 1)
    rows = user * SIDE + lax.broadcasted_iota(jnp.int32, part.shape, 0)
    cols = item * 32 + lax.broadcasted_iota(jnp.int32, part.shape, 1)
    return tail * scale, jnp.where(rows == cols, jnp.float32(0.0), part * scale)


def solution(mesh):
    both = P(("user", "item"), None)
    return jax.shard_map(
        local,
        mesh=mesh,
        in_specs=(both, both, P("user", "item", None), P("user", "item"), P("user", "item"),
                  P("user", "item", None), P("user", "item"), P("user", "item")),
        out_specs=(P("user", "item"), P("user", "item")),
        check_vma=False,
    )
```

```python
import jax
import jax.numpy as jnp
from jax import lax
from jax.experimental import pallas as pl
from jax.experimental.pallas import tpu as pltpu
from jax.sharding import PartitionSpec as P

SIDE = 128
BLOCKS = 16
COLS = 25
ZERO = 64
NA, NB = 7, 6
NK = NA + NB
MESH = pl.DeviceIdType.MESH
F32, BF16 = jnp.float32, jnp.bfloat16


def merge_kernel(up, ap, ub, ab, ur, uc, ar, ac, u_out, blk_out, map_out, acc):
    for t, pan in enumerate((up, ap)):
        for m in range(8):
            u_out[m % 2, t, :, (m // 2) * 128:(m // 2 + 1) * 128] = pan[:, m * 128:(m + 1) * 128]
    for row in range(4):
        for c in range(COLS + 1):
            map_out[row, c] = ZERO
    for t, (blk, rows, cols) in enumerate(((ub, ur, uc), (ab, ar, ac))):
        twin = [jnp.int32(0)] * BLOCKS
        for q in range(BLOCKS - 1, -1, -1):
            row, c = t * 2 + rows[0, q], cols[0, q]
            twin[q] = map_out[row, c]
            map_out[row, c] = t * BLOCKS + q
        for q in range(BLOCKS):
            blk_out[t * BLOCKS + q] = blk[q]
        for q in range(BLOCKS - 1):
            row, c = t * 2 + rows[0, q], cols[0, q]
            first = jnp.logical_and(map_out[row, c] == t * BLOCKS + q, twin[q] != ZERO)

            @pl.when(first)
            def _(q=q, t=t, blk=blk, rows=rows, cols=cols):
                acc[...] = blk[q].astype(F32)

                def add(o, carry):
                    same = jnp.logical_and(rows[0, o] == rows[0, q], cols[0, o] == cols[0, q])

                    @pl.when(same)
                    def _():
                        acc[...] += blk[o].astype(F32)

                    return carry

                lax.fori_loop(q + 1, BLOCKS, add, 0)
                blk_out[t * BLOCKS + q] = acc[...].astype(BF16)


def gram_kernel(u_ref, blk_ref, map_ref, tail_ref, self_ref, w_ref,
                g, xb, smap, vmap, tall, pt, srhs, rhs,
                far, near_p, near_m, keep_p, keep_m, own, rfar_p, rfar_m, rp, rm,
                wrow, wsend, wrelay, wp, wm,
                loc, xs, xr, zs, zr, ss, sr, bs, br, es, er, fs, fr, ns, nr, vs, vr):
    user, item = lax.axis_index("user"), lax.axis_index("item")
    y, a = user // 2, user % 2
    z, h, c = item // 4, (item // 2) % 2, item % 2
    x = h * 2 + a

    def dev(dy=0, dx=0, dz=0, flip=False):
        yy, xx, zz = (y + dy + 4) % 4, (x + dx + 4) % 4, (z + dz + 8) % 8
        cc = 1 - c if flip else c
        return (yy * 2 + xx % 2, zz * 4 + (xx // 2) * 2 + cc)

    partner = (y * 2 + (1 - a), item)

    def send(src, dst, ssem, rsem, to):
        return pltpu.make_async_remote_copy(
            src_ref=src, dst_ref=dst, send_sem=ssem, recv_sem=rsem,
            device_id=to, device_id_type=MESH)

    barrier = pltpu.get_barrier_semaphore()
    for peer in (dev(dy=1), dev(dy=-1), dev(dx=1), dev(dx=-1), dev(dx=2), dev(dz=1), dev(dz=-1), dev(flip=True)):
        pl.semaphore_signal(barrier, inc=1, device_id=peer, device_id_type=MESH)
    pl.semaphore_wait(barrier, 8)

    x_copies = [
        send(u_ref.at[a], g.at[z, c, 0, h], xs.at[2], xr.at[2], dev(dx=2)),
        send(u_ref.at[1 - a], g.at[z, c, 1, h], xs.at[0], xr.at[0], dev(dx=1)),
        send(u_ref.at[1 - a], g.at[z, c, 1, h], xs.at[1], xr.at[1], dev(dx=-1)),
    ]
    for cp in x_copies:
        cp.start()
    map_copy = send(map_ref, vmap, bs.at[4], br.at[4], partner)
    map_copy.start()
    b_copies = [send(blk_ref.at[pl.ds(8 * i, 8)], xb.at[pl.ds(32 + 8 * i, 8)], bs.at[i], br.at[i], partner)
                for i in range(4)]
    for cp in b_copies:
        cp.start()
    own_u = pltpu.make_async_copy(u_ref.at[a], g.at[z, c, 0, h], loc.at[0])
    own_b = pltpu.make_async_copy(blk_ref, xb.at[pl.ds(0, 32)], loc.at[1])
    own_m = pltpu.make_async_copy(map_ref, smap.at[0], loc.at[2])
    for cp in (own_u, own_b, own_m):
        cp.start()
    xb[ZERO] = jnp.zeros((SIDE, SIDE), BF16)
    x_copies[1].wait_recv()
    x_copies[2].wait_recv()

    def ring(step, sub, up):
        zz = (z + 8 - step) % 8 if up else (z + step) % 8
        i = (step if up else 4 + step) * 2 + sub
        return send(g.at[zz, c, sub], g.at[zz, c, sub], zs.at[i], zr.at[i], dev(dz=1 if up else -1))

    def share(zz, i):
        return send(g.at[zz, c], g.at[zz, c], ss.at[i], sr.at[i], dev(flip=True))

    ups = [[ring(k, s, True) for s in range(2)] for k in range(4)]
    downs = [[ring(k, s, False) for s in range(2)] for k in range(3)]
    ups[0][1].start()
    downs[0][1].start()
    own_u.wait()
    x_copies[0].wait_recv()
    ups[0][0].start()
    downs[0][0].start()
    shares = [share(z, 0)]
    shares[0].start()
    for k in range(4):
        for s in (1, 0):
            ups[k][s].wait_recv()
            if k < 3:
                ups[k + 1][s].start()
                downs[k][s].wait_recv()
                if k < 2:
                    downs[k + 1][s].start()
        shares.append(share((z + 7 - k) % 8, 1 + k))
        shares[-1].start()
        if k < 3:
            shares.append(share((z + 1 + k) % 8, 5 + k))
            shares[-1].start()
    for cp in shares:
        cp.wait_recv()

    for rel in range(4):
        wrow[rel] = jnp.zeros((8, SIDE), F32)
    for side in range(2):
        for t in range(2):
            for i in range(32):
                tall[i * 8:(i + 1) * 8, :] = g[i // 4, i % 2, side, (i // 2) % 2, t].astype(F32)
            first = side * 512 + t * 256
            for rel in range(4):
                yb = (y + rel) % 4
                v = tall[:, pl.ds(pl.multiple_of(yb * SIDE, SIDE), SIDE)]
                squares = jnp.sum(v * v, axis=0, keepdims=True)
                vt = v.T
                if t == 1:
                    squares, vt = squares * 0.5, vt * 0.5
                wrow[rel] += jnp.broadcast_to(squares, (8, SIDE))
                pt[rel * SIDE:(rel + 1) * SIDE, first:first + 256] = vt.astype(BF16)

            @pl.when(z % 2 == a)
            def _():
                srhs[first:first + 256, :] = tall[:, pl.ds(pl.multiple_of((z // 2) * SIDE, SIDE), SIDE)].astype(BF16)

    wsend[0] = wrow[2]
    wsend[1] = wrow[3]
    w_far = send(wsend.at[0], wrelay, vs.at[0], vr.at[0], dev(dy=1))
    w_near_m = send(wsend.at[1], wm, vs.at[1], vr.at[1], dev(dy=-1))
    w_far.start()
    w_near_m.start()

    map_copy.wait_recv()
    got_map = pltpu.make_async_copy(vmap, smap.at[1], loc.at[3])
    got_map.start()
    own_b.wait()
    own_m.wait()
    got_map.wait()
    for cp in b_copies:
        cp.wait_recv()

    e_copies = [send(srhs.at[pl.ds(s * 512, 512)], srhs.at[pl.ds((1 - s) * 512, 512)], es.at[s], er.at[s], partner)
                for s in range(2)]

    @pl.when(z % 2 == a)
    def _():
        for cp in e_copies:
            cp.start()

    def far_copy(k, up):
        if up:
            return send(far.at[k], rfar_p.at[k], fs.at[k], fr.at[k], dev(dy=1))
        return send(far.at[k], rfar_m.at[k - NA], fs.at[k], fr.at[k], dev(dy=-1))

    def near_copy(k, up):
        if up:
            return send(near_p.at[k], rp.at[k], ns.at[k], nr.at[k], dev(dy=1))
        return send(near_m.at[k], rm.at[k], ns.at[NK + k], nr.at[NK + k], dev(dy=-1))

    def compute(k, up, last=False):
        for j in range(1 if last else 2):
            for p in range(8):
                at = smap[p // 4, p % 4, 2 * k + j]
                if p >= 4:
                    at = jnp.where(at == ZERO, ZERO, at + 32)
                rhs[p * SIDE:(p + 1) * SIDE, j * SIDE:(j + 1) * SIDE] = xb[at]
        if last:
            rhs[:, SIDE:2 * SIDE] = srhs[...]
        terms = jnp.dot(pt[...], rhs[...], preferred_element_type=F32)
        far[k] = terms[256:384].astype(BF16)
        far_copy(k, up).start()
        own[k] = terms[0:128]
        if up:
            near_m[k] = terms[384:512].astype(BF16)
            near_copy(k, False).start()
            keep_p[k] = terms[128:256]
        else:
            near_p[k] = terms[128:256].astype(BF16)
            near_copy(k, True).start()
            keep_m[k - NA] = terms[384:512]

    def both(i, carry):
        compute(i, True)
        compute(NA + i, False)
        return carry

    lax.fori_loop(0, NB - 1, both, 0)
    compute(NB - 1, True)
    compute(NA - 1, True)

    @pl.when(z % 2 != a)
    def _():
        for cp in e_copies:
            cp.wait_recv()

    compute(NK - 1, False, last=True)

    w_far.wait_recv()
    wsend[2] = wrow[1] + wrelay[...]
    w_near_p = send(wsend.at[2], wp, vs.at[2], vr.at[2], dev(dy=1))
    w_near_p.start()

    def relay_up(k):
        far_copy(k, True).wait_recv()
        near_p[k] = (keep_p[k] + rfar_p[k].astype(F32)).astype(BF16)
        near_copy(k, True).start()

    def relay_down(k):
        far_copy(k, False).wait_recv()
        near_m[k] = (keep_m[k - NA] + rfar_m[k - NA].astype(F32)).astype(BF16)
        near_copy(k, False).start()

    def relay(i, carry):
        relay_up(i)
        relay_down(NA + i)
        return carry

    lax.fori_loop(0, NB, relay, 0)
    relay_up(NA - 1)

    def total(k):
        near_copy(k, True).wait_recv()
        near_copy(k, False).wait_recv()
        return own[k] + (rp[k].astype(F32) + rm[k].astype(F32))

    def finish(k, carry):
        tail_ref[:, pl.ds(pl.multiple_of(k * 256, 256), 256)] = total(k)
        return carry

    lax.fori_loop(0, NK - 1, finish, 0)
    end = total(NK - 1)
    tail_ref[:, (NK - 1) * 256:] = end[:, :SIDE]
    self_ref[...] = end[:, SIDE:]
    w_near_m.wait_recv()
    w_near_p.wait_recv()
    w_ref[...] = wrow[0] + (wp[...] + wm[...])

    for cp in x_copies + shares + b_copies + [map_copy, w_far, w_near_m, w_near_p]:
        cp.wait_send()
    for cp in ups + downs:
        for part in cp:
            part.wait_send()

    @pl.when(z % 2 == a)
    def _():
        for cp in e_copies:
            cp.wait_send()

    def drain_a(k, carry):
        far_copy(k, True).wait_send()
        near_copy(k, True).wait_send()
        near_copy(k, False).wait_send()
        return carry

    def drain_b(k, carry):
        far_copy(k, False).wait_send()
        near_copy(k, True).wait_send()
        near_copy(k, False).wait_send()
        return carry

    lax.fori_loop(0, NA, drain_a, 0)
    lax.fori_loop(NA, NK, drain_b, 0)


def local(up, ap, ub, ur, uc, ab, ar, ac):
    vmem, smem = pl.BlockSpec(memory_space=pltpu.VMEM), pl.BlockSpec(memory_space=pltpu.SMEM)
    hbm = pl.BlockSpec(memory_space=pl.ANY)
    shape = jax.ShapeDtypeStruct
    u, blk, cells = pl.pallas_call(
        merge_kernel,
        out_shape=(shape((2, 2, 8, 512), BF16), shape((32, SIDE, SIDE), BF16), shape((8, 128), jnp.int32)),
        in_specs=[vmem] * 4 + [smem] * 4,
        out_specs=(vmem, vmem, smem),
        scratch_shapes=[pltpu.VMEM((SIDE, SIDE), F32)],
        name="merge",
    )(up, ap, ub, ab, ur.T, uc.T, ar.T, ac.T)
    vm, dma = pltpu.VMEM, pltpu.SemaphoreType.DMA
    width = (NK * 2 - 1) * SIDE
    tail, own_self, weight = pl.pallas_call(
        gram_kernel,
        out_shape=(shape((SIDE, width), F32), shape((SIDE, SIDE), F32), shape((8, SIDE), F32)),
        in_specs=[hbm, hbm, hbm],
        out_specs=(vmem, vmem, vmem),
        scratch_shapes=[
            vm((8, 2, 2, 2, 2, 8, 512), BF16),
            vm((ZERO + 1, SIDE, SIDE), BF16),
            pltpu.SMEM((2, 8, 128), jnp.int32),
            vm((8, 128), jnp.int32),
            vm((256, 512), F32),
            vm((512, 1024), BF16),
            vm((1024, SIDE), BF16),
            vm((1024, 256), BF16),
            vm((NK, SIDE, 256), BF16),
            vm((NK, SIDE, 256), BF16),
            vm((NK, SIDE, 256), BF16),
            vm((NA, SIDE, 256), F32),
            vm((NB, SIDE, 256), F32),
            vm((NK, SIDE, 256), F32),
            vm((NA, SIDE, 256), BF16),
            vm((NB, SIDE, 256), BF16),
            vm((NK, SIDE, 256), BF16),
            vm((NK, SIDE, 256), BF16),
            vm((4, 8, SIDE), F32),
            vm((3, 8, SIDE), F32),
            vm((8, SIDE), F32),
            vm((8, SIDE), F32),
            vm((8, SIDE), F32),
            dma((4,)), dma((3,)), dma((3,)), dma((14,)), dma((14,)), dma((8,)), dma((8,)),
            dma((5,)), dma((5,)), dma((2,)), dma((2,)), dma((NK,)), dma((NK,)),
            dma((2 * NK,)), dma((2 * NK,)), dma((3,)), dma((3,)),
        ],
        compiler_params=pltpu.CompilerParams(
            collective_id=0, has_side_effects=True, vmem_limit_bytes=62 * 1024 * 1024),
        name="gram",
    )(u, blk, cells)
    user, item = lax.axis_index("user"), lax.axis_index("item")
    scale = lax.rsqrt(weight[0] + 1.0)[:, None]
    part = lax.dynamic_slice_in_dim(own_self, (item % 4) * 32, 32, 1)
    rows = user * SIDE + lax.broadcasted_iota(jnp.int32, part.shape, 0)
    cols = item * 32 + lax.broadcasted_iota(jnp.int32, part.shape, 1)
    return tail * scale, jnp.where(rows == cols, jnp.float32(0.0), part * scale)


def solution(mesh):
    both = P(("user", "item"), None)
    return jax.shard_map(
        local,
        mesh=mesh,
        in_specs=(both, both, P("user", "item", None), P("user", "item"), P("user", "item"),
                  P("user", "item", None), P("user", "item"), P("user", "item")),
        out_specs=(P("user", "item"), P("user", "item")),
        check_vma=False,
    )
```

```python
import jax
import jax.numpy as jnp
from jax import lax
from jax.experimental import pallas as pl
from jax.experimental.pallas import tpu as pltpu
from jax.sharding import PartitionSpec as P

SIDE = 128
BLOCKS = 16
COLS = 25
ZERO = 64
NK = 13
MESH = pl.DeviceIdType.MESH
F32, BF16 = jnp.float32, jnp.bfloat16


def merge_kernel(up, ap, ub, ab, ur, uc, ar, ac, u_out, blk_out, map_out, acc):
    for t, pan in enumerate((up, ap)):
        for m in range(8):
            u_out[m, t] = pan[:, m * 128:(m + 1) * 128]
    for row in range(4):
        for c in range(COLS + 1):
            map_out[row, c] = ZERO
    for t, (blk, rows, cols) in enumerate(((ub, ur, uc), (ab, ar, ac))):
        twin = [jnp.int32(0)] * BLOCKS
        for q in range(BLOCKS - 1, -1, -1):
            row, c = t * 2 + rows[0, q], cols[0, q]
            twin[q] = map_out[row, c]
            map_out[row, c] = t * BLOCKS + q
        for q in range(BLOCKS):
            blk_out[t * BLOCKS + q] = blk[q]
        for q in range(BLOCKS - 1):
            row, c = t * 2 + rows[0, q], cols[0, q]
            first = jnp.logical_and(map_out[row, c] == t * BLOCKS + q, twin[q] != ZERO)

            @pl.when(first)
            def _(q=q, t=t, blk=blk, rows=rows, cols=cols):
                acc[...] = blk[q].astype(F32)

                def add(o, carry):
                    same = jnp.logical_and(rows[0, o] == rows[0, q], cols[0, o] == cols[0, q])

                    @pl.when(same)
                    def _():
                        acc[...] += blk[o].astype(F32)

                    return carry

                lax.fori_loop(q + 1, BLOCKS, add, 0)
                blk_out[t * BLOCKS + q] = acc[...].astype(BF16)


def gram_kernel(u_ref, blk_ref, map_ref, tail_ref, self_ref, w_ref,
                g, hb, xb, smap, vmap, tall, pt, srhs, rhs,
                far, near, cross, keep, own, rfar, rnear, rcross,
                wrow, wsend, wrelay, wnear, wcross,
                loc, xs, xr, zs, zr, ss, sr, hs, hr, bs, br, fs, fr, ns, nr, cs, cr, vs, vr):
    user, item = lax.axis_index("user"), lax.axis_index("item")
    y, a = user // 2, user % 2
    z, h, c = item // 4, (item // 2) % 2, item % 2

    def across_x(v):
        return v + 1 - 2 * (v % 2)

    def inside_y(v):
        return v + 2 - 4 * ((v // 2) % 2)

    def across_y(v):
        return (3 - v // 2) * 2 + v % 2

    def e0(v):
        return across_x(v) + c * (inside_y(v) - across_x(v))

    def e1(v):
        return inside_y(v) + c * (across_x(v) - inside_y(v))

    e2 = across_y

    def owners(v):
        return [v, e1(v), e2(v), e2(e1(v))]

    partner = (e0(user), item)
    first, second = (e1(user), item), (e2(user), item)
    far_x = (user, z * 4 + (1 - h) * 2 + c)
    up_z, down_z = (user, (item + 4) % 32), (user, (item + 28) % 32)
    sibling = (user, item + 1 - 2 * c)

    def send(src, dst, ssem, rsem, to):
        return pltpu.make_async_remote_copy(
            src_ref=src, dst_ref=dst, send_sem=ssem, recv_sem=rsem,
            device_id=to, device_id_type=MESH)

    barrier = pltpu.get_barrier_semaphore()
    for peer in (partner, first, second, far_x, up_z, down_z, sibling):
        pl.semaphore_signal(barrier, inc=1, device_id=peer, device_id_type=MESH)
    pl.semaphore_wait(barrier, 7)

    x_copy = send(u_ref, g.at[z, c, h], xs.at[0], xr.at[0], far_x)
    x_copy.start()

    def ring(step, sub, up):
        zz = (z + 8 - step) % 8 if up else (z + step) % 8
        hh = h if sub == 0 else 1 - h
        i = (step if up else 4 + step) * 2 + sub
        src = u_ref if step == 0 and sub == 0 else g.at[zz, c, hh]
        return send(src, g.at[zz, c, hh], zs.at[i], zr.at[i], up_z if up else down_z)

    ups = [[ring(k, s, True) for s in range(2)] for k in range(4)]
    downs = [[ring(k, s, False) for s in range(2)] for k in range(3)]
    ups[0][0].start()
    downs[0][0].start()
    map_copy = send(map_ref, vmap, bs.at[4], br.at[4], partner)
    map_copy.start()
    b_copies = [send(blk_ref.at[pl.ds(8 * i, 8)], xb.at[pl.ds(32 + 8 * i, 8)], bs.at[i], br.at[i], partner)
                for i in range(4)]
    for cp in b_copies:
        cp.start()
    own_u = pltpu.make_async_copy(u_ref, g.at[z, c, h], loc.at[0])
    own_b = pltpu.make_async_copy(blk_ref, xb.at[pl.ds(0, 32)], loc.at[1])
    own_m = pltpu.make_async_copy(map_ref, smap.at[0], loc.at[2])
    for cp in (own_u, own_b, own_m):
        cp.start()
    xb[ZERO] = jnp.zeros((SIDE, SIDE), BF16)

    def share(zz, i):
        return send(g.at[zz, c], g.at[zz, c], ss.at[i], sr.at[i], sibling)

    theirs = owners(e0(user)) + [z]
    passed = []

    def pass_on(zz, cc, i):
        for n, block in enumerate(theirs):
            cp = send(g.at[zz, cc, :, block], hb.at[zz, cc, :, n], hs.at[i, n], hr.at[i, n], partner)
            cp.start()
            passed.append(cp)

    shares = []

    def spread(zz, i):
        cp = share(zz, i)
        cp.start()
        shares.append((cp, zz, i))
        pass_on(zz, c, i)

    seen = 0
    own_u.wait()
    x_copy.wait_recv()
    ups[0][1].start()
    downs[0][1].start()
    spread(z, 0)
    for k in range(4):
        for s in range(2):
            ups[k][s].wait_recv()
            if k < 3:
                ups[k + 1][s].start()
                downs[k][s].wait_recv()
                if k < 2:
                    downs[k + 1][s].start()
        ready = len(shares)
        spread((z + 7 - k) % 8, 1 + k)
        if k < 3:
            spread((z + 1 + k) % 8, 5 + k)
        for cp, zz, i in shares[seen:ready]:
            cp.wait_recv()
            pass_on(zz, 1 - c, 8 + i)
        seen = ready
    for cp, zz, i in shares[seen:]:
        cp.wait_recv()
        pass_on(zz, 1 - c, 8 + i)

    mine = owners(user)
    for rel in range(4):
        wrow[rel] = jnp.zeros((8, SIDE), F32)
    for side in range(2):
        if side == 1:
            for cp in passed:
                cp.wait_recv()
        for t in range(2):
            start = side * 512 + t * 256
            for n in range(5):
                for i in range(32):
                    zi, hi, ci = i // 4, (i // 2) % 2, i % 2
                    if side == 0:
                        block = mine[n] if n < 4 else z
                        piece = g[zi, ci, hi, block, t]
                    else:
                        piece = hb[zi, ci, hi, n, t]
                    tall[n, i * 8:(i + 1) * 8, :] = piece.astype(F32)
                v = tall[n]
                if n == 4:
                    srhs[start:start + 256, :] = v.astype(BF16)
                    continue
                squares = jnp.sum(v * v, axis=0, keepdims=True)
                vt = v.T
                if t == 1:
                    squares, vt = squares * 0.5, vt * 0.5
                wrow[n] += jnp.broadcast_to(squares, (8, SIDE))
                pt[n * SIDE:(n + 1) * SIDE, start:start + 256] = vt.astype(BF16)

    wsend[0] = wrow[3]
    wsend[1] = wrow[1]
    w_far = send(wsend.at[0], wrelay, vs.at[0], vr.at[0], first)
    w_near = send(wsend.at[1], wnear, vs.at[1], vr.at[1], first)
    w_far.start()
    w_near.start()

    map_copy.wait_recv()
    got_map = pltpu.make_async_copy(vmap, smap.at[1], loc.at[3])
    got_map.start()
    own_b.wait()
    own_m.wait()
    got_map.wait()
    for cp in b_copies:
        cp.wait_recv()

    def far_copy(k):
        return send(far.at[k], rfar.at[k], fs.at[k], fr.at[k], first)

    def near_copy(k):
        return send(near.at[k], rnear.at[k], ns.at[k], nr.at[k], first)

    def cross_copy(k):
        return send(cross.at[k], rcross.at[k], cs.at[k], cr.at[k], second)

    def compute(k, last=False):
        for j in range(1 if last else 2):
            for p in range(8):
                at = smap[p // 4, p % 4, 2 * k + j]
                if p >= 4:
                    at = jnp.where(at == ZERO, ZERO, at + 32)
                rhs[p * SIDE:(p + 1) * SIDE, j * SIDE:(j + 1) * SIDE] = xb[at]
        if last:
            rhs[:, SIDE:2 * SIDE] = srhs[...]
        terms = jnp.dot(pt[...], rhs[...], preferred_element_type=F32)
        far[k] = terms[384:512].astype(BF16)
        far_copy(k).start()
        near[k] = terms[128:256].astype(BF16)
        keep[k] = terms[256:384]
        own[k] = terms[0:128]

    def step(k, carry):
        compute(k)
        return carry

    lax.fori_loop(0, NK - 1, step, 0)
    compute(NK - 1, last=True)

    def start_near(k, carry):
        near_copy(k).start()
        return carry

    lax.fori_loop(0, NK, start_near, 0)

    w_far.wait_recv()
    wsend[2] = wrow[2] + wrelay[...]
    w_cross = send(wsend.at[2], wcross, vs.at[2], vr.at[2], second)
    w_cross.start()

    def relay(k, carry):
        far_copy(k).wait_recv()
        cross[k] = (keep[k] + rfar[k].astype(F32)).astype(BF16)
        cross_copy(k).start()
        return carry

    lax.fori_loop(0, NK, relay, 0)

    def total(k):
        near_copy(k).wait_recv()
        cross_copy(k).wait_recv()
        return own[k] + (rnear[k].astype(F32) + rcross[k].astype(F32))

    def finish(k, carry):
        tail_ref[:, pl.ds(pl.multiple_of(k * 256, 256), 256)] = total(k)
        return carry

    lax.fori_loop(0, NK - 1, finish, 0)
    end = total(NK - 1)
    tail_ref[:, (NK - 1) * 256:] = end[:, :SIDE]
    self_ref[...] = end[:, SIDE:].T
    w_near.wait_recv()
    w_cross.wait_recv()
    w_ref[...] = wrow[0] + (wnear[...] + wcross[...])

    for cp in [x_copy, map_copy, w_far, w_near, w_cross] + b_copies + passed:
        cp.wait_send()
    for cp, _, _ in shares:
        cp.wait_send()
    for pair in ups + downs:
        for cp in pair:
            cp.wait_send()

    def drain(k, carry):
        far_copy(k).wait_send()
        near_copy(k).wait_send()
        cross_copy(k).wait_send()
        return carry

    lax.fori_loop(0, NK, drain, 0)


def local(up, ap, ub, ur, uc, ab, ar, ac):
    vmem, smem = pl.BlockSpec(memory_space=pltpu.VMEM), pl.BlockSpec(memory_space=pltpu.SMEM)
    hbm = pl.BlockSpec(memory_space=pltpu.HBM)
    shape = jax.ShapeDtypeStruct
    u, blk, cells = pl.pallas_call(
        merge_kernel,
        out_shape=(shape((8, 2, 8, SIDE), BF16), shape((32, SIDE, SIDE), BF16), shape((8, 128), jnp.int32)),
        in_specs=[vmem] * 4 + [smem] * 4,
        out_specs=(vmem, vmem, smem),
        scratch_shapes=[pltpu.VMEM((SIDE, SIDE), F32)],
        compiler_params=pltpu.CompilerParams(vmem_limit_bytes=16 * 1024 * 1024),
        name="merge",
    )(up, ap, ub, ab, ur.T, uc.T, ar.T, ac.T)
    vm, dma = pltpu.VMEM, pltpu.SemaphoreType.DMA
    width = (NK * 2 - 1) * SIDE
    tail, own_self, weight = pl.pallas_call(
        gram_kernel,
        out_shape=(shape((SIDE, width), F32), shape((SIDE, SIDE), F32), shape((8, SIDE), F32)),
        in_specs=[hbm, hbm, hbm],
        out_specs=(vmem, vmem, vmem),
        scratch_shapes=[
            vm((8, 2, 2, 8, 2, 8, SIDE), BF16),
            vm((8, 2, 2, 5, 2, 8, SIDE), BF16),
            vm((ZERO + 1, SIDE, SIDE), BF16),
            pltpu.SMEM((2, 8, 128), jnp.int32),
            vm((8, 128), jnp.int32),
            vm((5, 256, SIDE), F32),
            vm((512, 1024), BF16),
            vm((1024, SIDE), BF16),
            vm((1024, 256), BF16),
            vm((NK, SIDE, 256), BF16),
            vm((NK, SIDE, 256), BF16),
            vm((NK, SIDE, 256), BF16),
            vm((NK, SIDE, 256), F32),
            vm((NK, SIDE, 256), F32),
            vm((NK, SIDE, 256), BF16),
            vm((NK, SIDE, 256), BF16),
            vm((NK, SIDE, 256), BF16),
            vm((4, 8, SIDE), F32),
            vm((3, 8, SIDE), F32),
            vm((8, SIDE), F32),
            vm((8, SIDE), F32),
            vm((8, SIDE), F32),
            dma((4,)), dma((1,)), dma((1,)), dma((14,)), dma((14,)), dma((8,)), dma((8,)),
            dma((16, 5)), dma((16, 5)), dma((5,)), dma((5,)),
            dma((NK,)), dma((NK,)), dma((NK,)), dma((NK,)), dma((NK,)), dma((NK,)), dma((3,)), dma((3,)),
        ],
        compiler_params=pltpu.CompilerParams(
            collective_id=0, has_side_effects=True, vmem_limit_bytes=32 * 1024 * 1024),
        name="gram",
    )(u, blk, cells)
    user, item = lax.axis_index("user"), lax.axis_index("item")
    scale = lax.rsqrt(weight[0] + 1.0)
    part = lax.dynamic_slice_in_dim(own_self, (item % 4) * 32, 32, 0)
    rows = user * SIDE + lax.broadcasted_iota(jnp.int32, part.shape, 1)
    cols = item * 32 + lax.broadcasted_iota(jnp.int32, part.shape, 0)
    part = jnp.where(rows == cols, jnp.float32(0.0), part * scale[None, :])
    return tail * scale[:, None], part.T


def solution(mesh):
    both = P(("user", "item"), None)
    return jax.shard_map(
        local,
        mesh=mesh,
        in_specs=(both, both, P("user", "item", None), P("user", "item"), P("user", "item"),
                  P("user", "item", None), P("user", "item"), P("user", "item")),
        out_specs=(P("user", "item"), P("user", "item")),
        check_vma=False,
    )
```
